32 devices in a mesh: row: 8 (over y, x, core), col: 4 (over z).
Axes of the slice: x: 2, y: 2, z: 4, core: 2. Of those that a mesh axis runs over, the one named last changes fastest.
Arguments:
- sparse_tiles: bfloat16 [128, 7, 128, 128], P(('row', 'col')), may hold values from -0.125 to 0.125
- tile_columns: int32 [128, 7], P(('row', 'col')), may hold values from 0 to 7, as said below
- block_counts: int32 [128], P(('row', 'col')), may hold values from 1 to 7, as said below
- krylov_first: bfloat16 [4096, 256], P(('row', 'col')), may hold values from -6 to 6
- panel_block: bfloat16 [4096, 256], P(('row', 'col')), may hold values from -1 to 1
Outputs:
- triangle_factor: float32 [256, 256], replicated
- coefficients: float32 [256, 768], replicated
- projected: bfloat16 [4096, 768], P(('row', 'col'))
The draws below stay inside these ranges and needn't reach their ends.
Inputs may be any that keep to these rules, and one draw needn't show every extreme that they name: `tile_columns`: distinct along the last dimension. `block_counts`: some aligned block of 4 entries holds 7 in every entry.
All inputs are finite; a program needn't handle non-finite values.
Results may differ from the reference program's by a relative error of at most 0.0049.
Values may be sent and summed in bfloat16 or wider, within the bound.
A program may use at most 64 MiB of HBM per device.

```python
import math
import jax
import jax.numpy as jnp
from jax import lax

PANEL = 256
TILE = 128
DEG_MAX = 7
ROWS_DEV = 128
NODES = 4096
RB_LOC = 4
CB_LOC = 8
N_ROW = 8
N_COL = 4


def draw_panel_block(key, part):
    first, second = jax.random.split(jax.random.fold_in(key, 11), 2)
    normal_part = jax.random.normal(first, (NODES, PANEL), jnp.float32)
    mixing = jnp.eye(PANEL, dtype=jnp.float32) + 0.6 * PANEL ** (-0.5) * jax.random.normal(second, (PANEL, PANEL), jnp.float32)
    values = jnp.dot(normal_part, mixing)
    rising = 1.0 + 2.0 * jnp.arange(NODES, dtype=jnp.float32) / NODES
    values = values * rising[:, None]
    values = values / math.sqrt(NODES)
    return jnp.clip(values, -1.0, 1.0).astype(jnp.bfloat16)


def draw_tile_columns(key, part):
    slot_rows = NODES * N_COL // TILE
    subkeys = jax.random.split(jax.random.fold_in(key, 21), slot_rows)

    def pick_order(subkey):
        return jax.random.permutation(subkey, CB_LOC)
    orders = jax.vmap(pick_order)(subkeys)
    return orders[:, :DEG_MAX].astype(jnp.int32)


def draw_block_counts(key, part):
    first, second, third = jax.random.split(jax.random.fold_in(key, 31), 3)
    base = jax.random.randint(first, (N_ROW, N_COL, RB_LOC), 1, 4)
    heavy = jax.random.randint(second, (N_ROW, 1, RB_LOC), 0, 4)
    factor = jnp.where(heavy == 3, 3, 1)
    counts = jnp.minimum(base * factor, DEG_MAX)
    fullest = jax.random.randint(third, (), 0, N_ROW * N_COL)
    flat = counts.reshape(N_ROW * N_COL, RB_LOC)
    marked = jnp.arange(N_ROW * N_COL) == fullest
    flat = jnp.where(marked[:, None], DEG_MAX, flat)
    return flat.reshape(-1).astype(jnp.int32)


def levels(stream_key, dims, cuts, least, top_value):
    level, own = 1.0, jax.random.fold_in(stream_key, 6)
    for dim, shards_of in cuts:
        draws = jnp.exp(jax.random.uniform(jax.random.fold_in(own, dim), (shards_of,), jnp.float32, least / len(cuts), top_value / len(cuts)))
        level = level * jnp.repeat(draws, dims[dim] // shards_of).reshape([-1 if axis == dim else 1 for axis in range(len(dims))])
    return level


def scatter_about(own_key, extent, spread, most, pieces=(), kind=jnp.bfloat16):
    gain = levels(own_key, extent, pieces, -0.22, 0.18) if pieces else 1.0
    drawn = jax.random.normal(own_key, extent, jnp.float32) * spread * gain
    return jnp.minimum(jnp.maximum(drawn, -most), most).astype(kind)


def setup_inputs(seed: int = 0) -> dict:
    key_list = jax.random.split(jax.random.key(seed), 6)
    return {
        "sparse_tiles": scatter_about(key_list[0], (NODES * N_COL // TILE, DEG_MAX, TILE, TILE), (TILE * DEG_MAX * N_COL // 2) ** -0.5, 0.125, ((0, 32),)),
        "tile_columns": draw_tile_columns(jax.random.fold_in(key_list[5], 71), 0),
        "block_counts": draw_block_counts(jax.random.fold_in(key_list[5], 71), 0),
        "krylov_first": scatter_about(key_list[3], (NODES, PANEL), 1.0, 6.0, ((0, 32),)),
        "panel_block": draw_panel_block(jax.random.fold_in(key_list[5], 71), 0),
    }


def factor_small(block):
    order = block.shape[0]
    positions = lax.broadcasted_iota(jnp.int32, (order,), 0)

    def one_column(index, state):
        working, lower, inverse = state
        column = lax.dynamic_slice_in_dim(working, index, 1, 1)[:, 0]
        pivot = jnp.sqrt(lax.dynamic_slice_in_dim(column, index, 1, 0)[0])
        column = jnp.where(positions >= index, column / pivot, jnp.zeros((), column.dtype))
        lower = lax.dynamic_update_slice_in_dim(lower, column[:, None], index, 1)
        working = working - column[:, None] * column[None, :]
        new_row = lax.dynamic_slice_in_dim(inverse, index, 1, 0) / pivot
        below = jnp.where(positions > index, column, jnp.zeros((), column.dtype))
        inverse = inverse - below[:, None] * new_row
        inverse = lax.dynamic_update_slice_in_dim(inverse, new_row, index, 0)
        return (working, lower, inverse)
    start = (block, jnp.zeros_like(block), jnp.eye(order, dtype=block.dtype))
    _, lower, inverse = lax.fori_loop(0, order, one_column, start)
    return (lower, inverse)

def factor_panel(gram_matrix):
    order = gram_matrix.shape[0]
    width = order // 4
    working = gram_matrix
    column_blocks = []
    diag_inverses = []
    for block_index in range(4):
        low = block_index * width
        lower_diag, inverse_diag = factor_small(working[:width, :width])
        under = jnp.dot(working[width:, :width], inverse_diag.T, precision=lax.Precision.HIGHEST)
        working = working[width:, width:] - jnp.dot(under, under.T, precision=lax.Precision.HIGHEST)
        column_blocks.append(jnp.concatenate([jnp.zeros((low, width), gram_matrix.dtype), lower_diag, under], axis=0))
        diag_inverses.append(inverse_diag)
    lower = jnp.concatenate(column_blocks, axis=1)
    identity = jnp.eye(order, dtype=gram_matrix.dtype)
    inverse_rows = []
    for block_index in range(4):
        low = block_index * width
        high = low + width
        target = identity[low:high, :]
        if block_index > 0:
            earlier = jnp.concatenate(inverse_rows, axis=0)
            target = target - jnp.dot(lower[low:high, :low], earlier, precision=lax.Precision.HIGHEST)
        inverse_rows.append(jnp.dot(diag_inverses[block_index], target, precision=lax.Precision.HIGHEST))
    return (lower, jnp.concatenate(inverse_rows, axis=0))

def multiply(source, sparse_tiles, tile_columns, block_counts):
    columns = source.shape[1]
    blocks = source.reshape(N_ROW, N_COL, ROWS_DEV, columns)
    by_column = jnp.transpose(blocks, (1, 0, 2, 3)).reshape(N_COL, CB_LOC, TILE, columns)
    tile_grid = sparse_tiles.reshape(N_ROW, N_COL, RB_LOC, DEG_MAX, TILE, TILE)
    column_grid = tile_columns.reshape(N_ROW, N_COL, RB_LOC, DEG_MAX)
    count_grid = block_counts.reshape(N_ROW, N_COL, RB_LOC)
    slot_index = lax.broadcasted_iota(jnp.int32, (RB_LOC, DEG_MAX), 1)

    def one_row(row_index):

        def one_column(running, col_index):
            picked = jnp.take(by_column[col_index], column_grid[row_index, col_index], axis=0)
            active = slot_index < count_grid[row_index, col_index][:, None]
            picked = jnp.where(active[:, :, None, None], picked.astype(jnp.float32), jnp.zeros((), jnp.float32))
            tile_term = jnp.einsum('bkij,bkjw->biw', tile_grid[row_index, col_index].astype(jnp.float32), picked)
            return (running + tile_term, None)
        start = jnp.zeros((RB_LOC, TILE, columns), jnp.float32)
        summed, _ = lax.scan(one_column, start, jnp.arange(N_COL, dtype=jnp.int32))
        return summed.reshape(RB_LOC * TILE, columns)
    rows_all = lax.map(one_row, jnp.arange(N_ROW, dtype=jnp.int32))
    return rows_all.reshape(NODES, columns).astype(jnp.bfloat16)

def reference(sparse_tiles, tile_columns, block_counts, krylov_first, panel_block):
    krylov_second = multiply(krylov_first, sparse_tiles, tile_columns, block_counts)
    krylov_third = multiply(krylov_second, sparse_tiles, tile_columns, block_counts)
    trailing = jnp.concatenate([krylov_first, krylov_second, krylov_third], axis=1)
    gram_matrix = jnp.dot(panel_block.T, panel_block, preferred_element_type=jnp.float32)
    cross_terms = jnp.dot(panel_block.T, trailing, preferred_element_type=jnp.float32)
    lower_factor, lower_inverse = factor_panel(gram_matrix)
    coefficients = jnp.dot(lower_inverse, cross_terms, precision=lax.Precision.HIGHEST)
    weights = jnp.dot(lower_inverse.T, coefficients, precision=lax.Precision.HIGHEST)
    removed = jnp.dot(panel_block.astype(jnp.float32), weights, precision=lax.Precision.HIGHEST)
    projected = (trailing.astype(jnp.float32) - removed).astype(jnp.bfloat16)
    return (lower_factor.T, coefficients, projected)
```

```python
import functools

import jax
import jax.numpy as jnp
from jax import lax
from jax.experimental import pallas as pl
from jax.experimental.pallas import tpu as pltpu
from jax.sharding import PartitionSpec as P

HIGHEST = lax.Precision.HIGHEST
F32 = jnp.float32
BF16 = jnp.bfloat16


def dot_nn(a, b, precision=None):
    return lax.dot_general(a, b, (((1,), (0,)), ((), ())), precision=precision, preferred_element_type=F32)


def dot_nt(a, b, precision=None):
    return lax.dot_general(a, b, (((1,), (1,)), ((), ())), precision=precision, preferred_element_type=F32)


def dot_tn(a, b, precision=None):
    return lax.dot_general(a, b, (((0,), (0,)), ((), ())), precision=precision, preferred_element_type=F32)


def eliminate(diag, work_ref, out_ref):
    width = diag.shape[0]
    low = lax.broadcasted_iota(jnp.int32, (width, width), 0)
    high = lax.broadcasted_iota(jnp.int32, (width, width), 1)
    work_ref[...] = jnp.concatenate([diag, (low == high).astype(F32)], axis=1)
    sub = lax.broadcasted_iota(jnp.int32, (8, 2 * width), 0)

    def group(index, carry):
        rows = work_ref[:8, :]
        scale = jnp.zeros((8, 2 * width), F32)
        spread = [jnp.broadcast_to(rows[:, k : k + 1], (8, 2 * width)) for k in range(8)]
        for i in range(8):
            inverse = 1.0 / jnp.broadcast_to(spread[i][i : i + 1, :], (8, 2 * width))
            factor = jnp.where(sub > i, spread[i] * inverse, 0.0)
            scale = jnp.where(sub == i, inverse, scale)
            for k in range(i + 1, 8):
                spread[k] = spread[k] - factor * spread[k][i : i + 1, :]
            rows = rows - factor * rows[i : i + 1, :]
        scaled = rows * scale
        rest = work_ref[...] - dot_tn(scaled[:, :width], rows, HIGHEST)
        at = pl.multiple_of(index * 8, 8)
        out_ref[pl.ds(at, 8), :] = pltpu.roll(rows * jnp.sqrt(scale), index * 8, 1)
        rest = pltpu.roll(rest, 2 * width - 8, 1)
        work_ref[: width - 8, :] = rest[8:, :]
        work_ref[width - 8 :, :] = jnp.zeros((8, 2 * width), F32)
        return carry

    lax.fori_loop(0, width // 8, group, 0)
    both = out_ref[...]
    upper = jnp.where(high >= low, both[:, :width], 0.0)
    inverse = jnp.where(high <= low, both[:, width:], 0.0)
    return upper, inverse


def body(n_row, n_col, degree, row_blocks, tile,
         tiles_hbm, columns_ref, counts_ref, first_ref, panel_ref,
         upper_out, coef_out, proj_out,
         tiles_ref, gathered_a, gathered_b, sums_ref, send_a, send_b, get_a, get_b,
         second_ref, third_ref,
         part_0, part_1, part_2, take_0, take_1, take_2,
         mix_0, mix_1, mix_2, full_0, full_1, full_2,
         work_ref, out_ref, lower_ref,
         tile_sem, gs_sem, gr_sem, ss_sem, sr_sem, rs_sem, rr_sem, xs_sem, xr_sem, as_sem, ar_sem):
    row = lax.axis_index("row")
    col = lax.axis_index("col")
    panel_width = panel_ref.shape[1]
    rows_dev = panel_ref.shape[0]
    strip = panel_width // n_row

    load_tiles = pltpu.make_async_copy(tiles_hbm, tiles_ref, tile_sem)
    load_tiles.start()

    def row_peer(step):
        return lax.rem(row + step, n_row)

    def col_peer(step):
        return lax.rem(col + step, n_col)

    barrier = pltpu.get_barrier_semaphore()
    for step in range(1, n_row):
        pl.semaphore_signal(barrier, inc=1, device_id=(row_peer(step), col), device_id_type=pl.DeviceIdType.MESH)
    for step in range(1, n_col):
        pl.semaphore_signal(barrier, inc=1, device_id=(row, col_peer(step)), device_id_type=pl.DeviceIdType.MESH)

    def over_row(source, target, send_sem, recv_sem):
        copies = []
        for step in range(1, n_row):
            peer = row_peer(step)
            copies.append(pltpu.make_async_remote_copy(
                src_ref=source(step, peer), dst_ref=target(step, peer),
                send_sem=send_sem.at[step], recv_sem=recv_sem.at[step],
                device_id=(peer, col), device_id_type=pl.DeviceIdType.MESH))
        return copies

    def over_col(source, target, send_sem, recv_sem):
        copies = []
        for step in range(1, n_col):
            peer = col_peer(step)
            copies.append(pltpu.make_async_remote_copy(
                src_ref=source(step, peer), dst_ref=target(step, peer),
                send_sem=send_sem.at[step], recv_sem=recv_sem.at[step],
                device_id=(row, peer), device_id_type=pl.DeviceIdType.MESH))
        return copies

    def start(copies):
        for copy in copies:
            copy.start()

    def arrive(copies):
        for copy in copies:
            copy.wait_recv()

    def gather(source_ref, gathered_ref, index):
        copies = over_row(lambda s, p: source_ref, lambda s, p: gathered_ref.at[row],
                          gs_sem.at[index], gr_sem.at[index])
        start(copies)
        gathered_ref[row] = source_ref[...]
        return copies

    def product(gathered_ref, send_ref):
        for b in range(row_blocks):
            left, right = [], []
            for k in range(degree):
                live = k < counts_ref[0, b]
                value = tiles_ref[b, k]
                left.append(jnp.where(live, value, jnp.zeros_like(value)))
                right.append(gathered_ref[columns_ref[b, k]])
            total = dot_nn(jnp.concatenate(left, axis=1), jnp.concatenate(right, axis=0))
            sums_ref[b * tile : (b + 1) * tile, :] = total
        for c in range(n_col):
            send_ref[c] = sums_ref[c * rows_dev : (c + 1) * rows_dev, :].astype(BF16)

    def scatter(send_ref, get_ref, index):
        copies = over_col(lambda s, p: send_ref.at[p], lambda s, p: get_ref.at[s],
                          ss_sem.at[index], sr_sem.at[index])
        start(copies)
        return copies

    def collect(copies, get_ref, result_ref):
        own = sums_ref[pl.ds(pl.multiple_of(col * rows_dev, 8), rows_dev), :]
        arrive(copies)
        for step in range(1, n_col):
            own = own + get_ref[step].astype(F32)
        result_ref[...] = own.astype(BF16)

    def reduce_row(value_parts, part_ref, take_ref, index):
        at = 0
        for value in value_parts:
            width = value.shape[1]
            part_ref[:, :, at : at + width] = value.reshape(n_row, strip, width)
            at += width
        copies = over_row(lambda s, p: part_ref.at[p], lambda s, p: take_ref.at[s],
                          rs_sem.at[index], rr_sem.at[index])
        start(copies)
        return copies

    def exchange_col(copies, part_ref, take_ref, mix_ref, index):
        total = part_ref[row]
        arrive(copies)
        for step in range(1, n_row):
            total = total + take_ref[step]
        mix_ref[col] = total
        copies = over_col(lambda s, p: mix_ref.at[col], lambda s, p: mix_ref.at[col],
                          xs_sem.at[index], xr_sem.at[index])
        start(copies)
        return copies

    def share_row(copies, mix_ref, full_ref, index):
        arrive(copies)
        total = mix_ref[0]
        for c in range(1, n_col):
            total = total + mix_ref[c]
        full_ref[row] = total
        copies = over_row(lambda s, p: full_ref.at[row], lambda s, p: full_ref.at[row],
                          as_sem.at[index], ar_sem.at[index])
        start(copies)
        return copies

    panel = panel_ref[...]
    gram_local = dot_tn(panel, panel)
    pl.semaphore_wait(barrier, n_row - 1 + n_col - 1)

    sent = []
    reduce_0 = reduce_row([gram_local], part_0, take_0, 0)
    gather_1 = gather(first_ref, gathered_a, 0)
    first_local = dot_tn(panel, first_ref[...])
    exchange_0 = exchange_col(reduce_0, part_0, take_0, mix_0, 0)
    load_tiles.wait()
    arrive(gather_1)
    product(gathered_a, send_a)
    scatter_1 = scatter(send_a, get_a, 0)
    share_0 = share_row(exchange_0, mix_0, full_0, 0)
    collect(scatter_1, get_a, second_ref)
    gather_2 = gather(second_ref, gathered_b, 1)
    reduce_1 = reduce_row([first_local, dot_tn(panel, second_ref[...])], part_1, take_1, 1)
    arrive(share_0)
    gram = full_0[...].reshape(panel_width, panel_width)
    pieces = 4
    width = panel_width // pieces
    columns = [gram[width * j :, width * j : width * (j + 1)] for j in range(pieces)]
    uppers, inverses, unders = [], [], []

    def factor(b):
        upper, inverse = eliminate(columns[b][:width], work_ref, out_ref)
        under = None
        if b < pieces - 1:
            under = dot_nt(columns[b][width:], inverse, HIGHEST)
            for j in range(b + 1, pieces):
                o = (j - b - 1) * width
                columns[j] = columns[j] - dot_nt(under[o:], under[o : o + width], HIGHEST)
        uppers.append(upper)
        inverses.append(inverse)
        unders.append(under)

    arrive(gather_2)
    product(gathered_b, send_b)
    scatter_2 = scatter(send_b, get_b, 1)
    exchange_1 = exchange_col(reduce_1, part_1, take_1, mix_1, 1)
    factor(0)
    collect(scatter_2, get_b, third_ref)
    reduce_2 = reduce_row([dot_tn(panel, third_ref[...])], part_2, take_2, 2)
    share_1 = share_row(exchange_1, mix_1, full_1, 1)
    factor(1)
    exchange_2 = exchange_col(reduce_2, part_2, take_2, mix_2, 2)
    factor(2)
    share_2 = share_row(exchange_2, mix_2, full_2, 2)
    factor(3)

    identity = (lax.broadcasted_iota(jnp.int32, (width, panel_width), 1)
                - lax.broadcasted_iota(jnp.int32, (width, panel_width), 0))
    for b in range(pieces):
        target = (identity == b * width).astype(F32)
        for e in range(b):
            o = (b - e - 1) * width
            target = target - dot_nn(unders[e][o : o + width], lower_ref[e * width : (e + 1) * width, :], HIGHEST)
        lower_ref[b * width : (b + 1) * width, :] = dot_nn(inverses[b], target, HIGHEST)
    for b in range(pieces):
        parts = [jnp.zeros((width, b * width), F32)] if b else []
        parts.append(uppers[b])
        if b < pieces - 1:
            parts.append(unders[b].T)
        upper_out[b * width : (b + 1) * width, :] = jnp.concatenate(parts, axis=1)

    def finish(full_ref, sources, at):
        lower_inverse = lower_ref[...]
        cross = full_ref[...].reshape(panel_width, full_ref.shape[2])
        coefficients = dot_nn(lower_inverse, cross, HIGHEST)
        coef_out[:, at : at + cross.shape[1]] = coefficients
        weights = dot_tn(lower_inverse, coefficients, HIGHEST)
        weight_high = weights.astype(BF16)
        weight_rest = (weights - weight_high.astype(F32)).astype(BF16)
        removed = dot_nn(panel_ref[...], weight_high) + dot_nn(panel_ref[...], weight_rest)
        for j, source in enumerate(sources):
            here = removed[:, j * panel_width : (j + 1) * panel_width]
            low = at + j * panel_width
            proj_out[:, low : low + panel_width] = (source[...].astype(F32) - here).astype(BF16)

    arrive(share_1)
    finish(full_1, [first_ref, second_ref], 0)
    arrive(share_2)
    finish(full_2, [third_ref], 2 * panel_width)

    for copies in (reduce_0, gather_1, exchange_0, scatter_1, share_0, gather_2, reduce_1, scatter_2,
                   exchange_1, reduce_2, share_1, exchange_2, share_2):
        for copy in copies:
            copy.wait_send()


def shards(n_row, n_col, sparse_tiles, tile_columns, block_counts, krylov_first, panel_block):
    row_blocks, degree, tile, _ = sparse_tiles.shape
    rows_dev, width = panel_block.shape
    strip = width // n_row
    vmem = pl.BlockSpec(memory_space=pltpu.VMEM)
    smem = pl.BlockSpec(memory_space=pltpu.SMEM)
    call = pl.pallas_call(
        functools.partial(body, n_row, n_col, degree, row_blocks, tile),
        out_shape=[
            jax.ShapeDtypeStruct((width, width), F32),
            jax.ShapeDtypeStruct((width, 3 * width), F32),
            jax.ShapeDtypeStruct((rows_dev, 3 * width), BF16),
        ],
        in_specs=[pl.BlockSpec(memory_space=pl.ANY), smem, smem, vmem, vmem],
        out_specs=[vmem, vmem, vmem],
        scratch_shapes=[
            pltpu.VMEM(sparse_tiles.shape, BF16),
            pltpu.VMEM((n_row, rows_dev, width), BF16),
            pltpu.VMEM((n_row, rows_dev, width), BF16),
            pltpu.VMEM((row_blocks * tile, width), F32),
            pltpu.VMEM((n_col, rows_dev, width), BF16),
            pltpu.VMEM((n_col, rows_dev, width), BF16),
            pltpu.VMEM((n_col, rows_dev, width), BF16),
            pltpu.VMEM((n_col, rows_dev, width), BF16),
            pltpu.VMEM((rows_dev, width), BF16),
            pltpu.VMEM((rows_dev, width), BF16),
            *[pltpu.VMEM((n_row, strip, k * width), F32) for k in (1, 2, 1)],
            *[pltpu.VMEM((n_row, strip, k * width), F32) for k in (1, 2, 1)],
            *[pltpu.VMEM((n_col, strip, k * width), F32) for k in (1, 2, 1)],
            *[pltpu.VMEM((n_row, strip, k * width), F32) for k in (1, 2, 1)],
            pltpu.VMEM((width // 4, width // 2), F32),
            pltpu.VMEM((width // 4, width // 2), F32),
            pltpu.VMEM((width, width), F32),
            pltpu.SemaphoreType.DMA,
            *[pltpu.SemaphoreType.DMA((2, n_row))] * 2,
            *[pltpu.SemaphoreType.DMA((2, n_col))] * 2,
            *[pltpu.SemaphoreType.DMA((3, n_row))] * 2,
            *[pltpu.SemaphoreType.DMA((3, n_col))] * 2,
            *[pltpu.SemaphoreType.DMA((3, n_row))] * 2,
        ],
        compiler_params=pltpu.CompilerParams(collective_id=0, has_side_effects=True),
        name="range_finder",
    )
    return tuple(call(sparse_tiles, tile_columns, block_counts.reshape(1, row_blocks), krylov_first, panel_block))


def solution(mesh):
    n_row, n_col = mesh.shape["row"], mesh.shape["col"]
    in_specs = (
        P(("row", "col"), None, None, None),
        P(("row", "col"), None),
        P(("row", "col")),
        P(("row", "col"), None),
        P(("row", "col"), None),
    )
    out_specs = (P(), P(), P(("row", "col"), None))
    return jax.shard_map(
        functools.partial(shards, n_row, n_col), mesh=mesh, in_specs=in_specs, out_specs=out_specs, check_vma=False
    )
```

```python
import functools

import jax
import jax.numpy as jnp
from jax import lax
from jax.experimental import pallas as pl
from jax.experimental.pallas import tpu as pltpu
from jax.sharding import PartitionSpec as P

HIGHEST = lax.Precision.HIGHEST
F32 = jnp.float32
BF16 = jnp.bfloat16


def dot_nn(a, b, precision=None):
    return lax.dot_general(a, b, (((1,), (0,)), ((), ())), precision=precision, preferred_element_type=F32)


def dot_nt(a, b, precision=None):
    return lax.dot_general(a, b, (((1,), (1,)), ((), ())), precision=precision, preferred_element_type=F32)


def dot_tn(a, b, precision=None):
    return lax.dot_general(a, b, (((0,), (0,)), ((), ())), precision=precision, preferred_element_type=F32)


def eliminate(diag, work_ref, out_ref):
    width = diag.shape[0]
    low = lax.broadcasted_iota(jnp.int32, (width, width), 0)
    high = lax.broadcasted_iota(jnp.int32, (width, width), 1)
    work_ref[...] = jnp.concatenate([diag, (low == high).astype(F32)], axis=1)
    sub = lax.broadcasted_iota(jnp.int32, (8, 2 * width), 0)

    def group(index, carry):
        rows = work_ref[:8, :]
        scale = jnp.zeros((8, 2 * width), F32)
        spread = [jnp.broadcast_to(rows[:, k : k + 1], (8, 2 * width)) for k in range(8)]
        for i in range(8):
            inverse = 1.0 / jnp.broadcast_to(spread[i][i : i + 1, :], (8, 2 * width))
            factor = jnp.where(sub > i, spread[i] * inverse, 0.0)
            scale = jnp.where(sub == i, inverse, scale)
            for k in range(i + 1, 8):
                spread[k] = spread[k] - factor * spread[k][i : i + 1, :]
            rows = rows - factor * rows[i : i + 1, :]
        scaled = rows * scale
        rest = work_ref[...] - dot_tn(scaled[:, :width], rows, HIGHEST)
        at = pl.multiple_of(index * 8, 8)
        out_ref[pl.ds(at, 8), :] = pltpu.roll(rows * jnp.sqrt(scale), index * 8, 1)
        rest = pltpu.roll(rest, 2 * width - 8, 1)
        work_ref[: width - 8, :] = rest[8:, :]
        work_ref[width - 8 :, :] = jnp.zeros((8, 2 * width), F32)
        return carry

    lax.fori_loop(0, width // 8, group, 0)
    both = out_ref[...]
    upper = jnp.where(high >= low, both[:, :width], 0.0)
    inverse = jnp.where(high <= low, both[:, width:], 0.0)
    return upper, inverse


def over_chunks(total, chunk, run):
    if total <= chunk:
        run(0, total)
    else:
        def one(index, carry):
            run(pl.multiple_of(index * chunk, chunk), chunk)
            return carry

        lax.fori_loop(0, total // chunk, one, 0)


def body(n_row, n_col, degree, row_blocks, tile,
         tiles_hbm, columns_ref, counts_ref, first_ref, panel_ref,
         lower_ref, upper_out, cross_out, second_ref, third_ref,
         tiles_ref, dense_ref, gathered_a, gathered_b, panels_ref, sums_ref, send_a, send_b, get_a, get_b,
         wing_ref, wing_core, wing_half, wing_take, wing_own,
         part_0, part_1, part_2, core_0, core_1, core_2, half_0, half_1, half_2, take_0, take_1, take_2,
         mix_0, mix_1, mix_2, full_0, full_1, full_2,
         work_ref, out_ref,
         tile_sem, gs_sem, gr_sem, gfs_sem, gfr_sem, ps_sem, pr_sem, ss_sem, sr_sem,
         cs_sem, cr_sem, rs_sem, rr_sem, xs_sem, xr_sem, as_sem, ar_sem, afs_sem, afr_sem):
    row = lax.axis_index("row")
    col = lax.axis_index("col")
    panel_width = panel_ref.shape[1]
    rows_dev = panel_ref.shape[0]
    n_chip = n_row // 2
    chip = row // 2
    core = lax.rem(row, 2)
    other = 1 - core
    partner = chip * 2 + other
    mesh_type = pl.DeviceIdType.MESH

    load_tiles = pltpu.make_async_copy(tiles_hbm, tiles_ref, tile_sem)
    load_tiles.start()

    def ahead(step):
        return lax.rem(chip + step, n_chip)

    def behind(step):
        return lax.rem(chip + n_chip - step, n_chip)

    def col_peer(step):
        return lax.rem(col + step, n_col)

    barrier = pltpu.get_barrier_semaphore()
    pl.semaphore_signal(barrier, inc=1, device_id=(partner, col), device_id_type=mesh_type)
    for step in range(1, n_chip):
        pl.semaphore_signal(barrier, inc=1, device_id=(ahead(step) * 2 + core, col), device_id_type=mesh_type)
    for step in range(1, n_col):
        pl.semaphore_signal(barrier, inc=1, device_id=(row, col_peer(step)), device_id_type=mesh_type)

    everything = []

    def begin(copies):
        for copy in copies:
            copy.start()
        everything.extend(copies)
        return copies

    def arrive(copies):
        for copy in copies:
            copy.wait_recv()

    def to_partner(source, target, send_sem, recv_sem):
        return pltpu.make_async_remote_copy(
            src_ref=source, dst_ref=target, send_sem=send_sem, recv_sem=recv_sem,
            device_id=(partner, col), device_id_type=mesh_type)

    def over_chips(source, target, send_sem, recv_sem):
        return [
            pltpu.make_async_remote_copy(
                src_ref=source(step), dst_ref=target(step),
                send_sem=send_sem.at[step], recv_sem=recv_sem.at[step],
                device_id=(ahead(step) * 2 + core, col), device_id_type=mesh_type)
            for step in range(1, n_chip)
        ]

    def over_col(source, target, send_sem, recv_sem):
        return [
            pltpu.make_async_remote_copy(
                src_ref=source(step), dst_ref=target(step),
                send_sem=send_sem.at[step], recv_sem=recv_sem.at[step],
                device_id=(row, col_peer(step)), device_id_type=mesh_type)
            for step in range(1, n_col)
        ]

    def gather(source, slots, sems):
        send, recv, pass_send, pass_recv = sems
        copies = begin(over_chips(lambda s: source, lambda s: slots(core, chip), send, recv))
        near = begin([to_partner(source, slots(core, chip), pass_send.at[0], pass_recv.at[0])])
        return copies, near

    def relay(state, slots, sems):
        copies, near = state
        send, recv, pass_send, pass_recv = sems
        passed = list(near)
        for step, copy in enumerate(copies, start=1):
            copy.wait_recv()
            here = slots(core, behind(step))
            passed += begin([to_partner(here, here, pass_send.at[step], pass_recv.at[step])])
        return passed

    def gather_sems(index):
        return gs_sem.at[index], gr_sem.at[index], gfs_sem.at[index], gfr_sem.at[index]

    def share_sems(index):
        return as_sem.at[index], ar_sem.at[index], afs_sem.at[index], afr_sem.at[index]

    def fold(part_ref, core_ref, index):
        return begin([to_partner(part_ref.at[other], core_ref, cs_sem.at[index], cr_sem.at[index])])

    def spread(folded, part_ref, core_ref, half_ref, take_ref, index):
        arrive(folded)
        half_ref[...] = (part_ref[core].astype(F32) + core_ref[...].astype(F32)).astype(half_ref.dtype)
        return begin(over_chips(lambda s: half_ref.at[ahead(s)], lambda s: take_ref.at[s],
                                rs_sem.at[index], rr_sem.at[index]))

    def strip_sum(copies, half_ref, take_ref):
        total = half_ref[chip].astype(F32)
        arrive(copies)
        for step in range(1, n_chip):
            total = total + take_ref[step].astype(F32)
        return total

    def put(value, part_ref, at):
        width = value.shape[1]
        part_ref[:, :, :, at : at + width] = value.reshape(part_ref.shape[:3] + (width,))

    def exchange(total, mix_ref, index):
        mix_ref[col] = total
        return begin(over_col(lambda s: mix_ref.at[col], lambda s: mix_ref.at[col],
                              xs_sem.at[index], xr_sem.at[index]))

    def share(copies, mix_ref, full_ref, index):
        arrive(copies)
        total = mix_ref[0]
        for c in range(1, n_col):
            total = total + mix_ref[c]
        full_ref[core, chip] = total
        return gather(full_ref.at[core, chip], lambda k, q: full_ref.at[k, q], share_sems(index))

    def whole(full_ref):
        return full_ref[...].reshape(panel_width, full_ref.shape[3])

    def product(gathered_ref, send_ref):
        right = gathered_ref[...].reshape(n_row * rows_dev, panel_width)

        def run(at, size):
            sums_ref[pl.ds(at, size), :] = dot_nn(dense_ref[pl.ds(at, size), :], right)

        over_chunks(row_blocks * tile, 4 * tile, run)
        for c in range(n_col):
            send_ref[c] = sums_ref[c * rows_dev : (c + 1) * rows_dev, :].astype(BF16)

    def scatter(send_ref, get_ref, index):
        return begin(over_col(lambda s: send_ref.at[col_peer(s)], lambda s: get_ref.at[s],
                              ss_sem.at[index], sr_sem.at[index]))

    def collect(copies, get_ref, result_ref):
        own = sums_ref[pl.ds(pl.multiple_of(col * rows_dev, 8), rows_dev), :]
        arrive(copies)
        for step in range(1, n_col):
            own = own + get_ref[step].astype(F32)
        result_ref[...] = own.astype(BF16)

    def slots_a(k, q):
        return gathered_a.at[q * 2 + k]

    def slots_b(k, q):
        return gathered_b.at[q * 2 + k]

    panel = panel_ref[...]
    put(dot_tn(panel, panel), part_0, 0)
    pl.semaphore_wait(barrier, n_chip + n_col - 1)

    fold_0 = fold(part_0, core_0, 0)
    gather_1 = gather(first_ref, slots_a, gather_sems(0))
    panels = begin(over_col(lambda s: panel_ref, lambda s: panels_ref.at[col], ps_sem, pr_sem))
    gathered_a[row] = first_ref[...]
    panels_ref[col] = panel_ref[...]
    spread_0 = spread(fold_0, part_0, core_0, half_0, take_0, 0)

    load_tiles.wait()
    column_blocks = n_row * rows_dev // tile

    def place(b):
        for j in range(column_blocks):
            slot = jnp.int32(0)
            live = jnp.int32(0)
            for k in range(degree):
                hit = jnp.logical_and(columns_ref[b, k] == j, k < counts_ref[0, b])
                slot = jnp.where(hit, k, slot)
                live = jnp.where(hit, 1, live)
            value = tiles_ref[b, slot]
            dense_ref[pl.ds(b * tile, tile), j * tile : (j + 1) * tile] = jnp.where(
                live > 0, value, jnp.zeros_like(value))

    if row_blocks <= 4:
        for b in range(row_blocks):
            place(b)
    else:
        def place_one(b, carry):
            place(b)
            return carry

        lax.fori_loop(0, row_blocks, place_one, 0)

    passed_1 = relay(gather_1, slots_a, gather_sems(0))
    put(dot_tn(panel, first_ref[...]), part_1, 0)
    fold_1 = fold(part_1, core_1, 1)
    arrive(passed_1)
    product(gathered_a, send_a)
    scatter_1 = scatter(send_a, get_a, 0)

    arrive(panels)
    rows_range = panels_ref[...].reshape(n_col * rows_dev, panel_width).T
    pair = 2 * rows_dev

    def wing(at, size):
        value = dot_nn(rows_range, dense_ref[:, pl.ds(at, size)]).astype(BF16)
        for e in range(size // pair):
            q = at // pair + e
            wing_ref[0, q] = value[:, e * pair : e * pair + rows_dev]
            wing_ref[1, q] = value[:, e * pair + rows_dev : (e + 1) * pair]

    over_chunks(n_row * rows_dev, 8 * rows_dev, wing)
    fold_3 = fold(wing_ref, wing_core, 3)
    exchange_0 = exchange(strip_sum(spread_0, half_0, take_0), mix_0, 0)
    spread_3 = spread(fold_3, wing_ref, wing_core, wing_half, wing_take, 3)
    spread_1 = spread(fold_1, part_1, core_1, half_1, take_1, 1)
    wing_own[...] = strip_sum(spread_3, wing_half, wing_take).astype(BF16)
    share_0 = share(exchange_0, mix_0, full_0, 0)
    collect(scatter_1, get_a, second_ref)
    gather_2 = gather(second_ref, slots_b, gather_sems(1))
    put(dot_tn(panel, second_ref[...]), part_2, 0)
    put(dot_nn(wing_own[...], second_ref[...]), part_2, panel_width)
    fold_2 = fold(part_2, core_2, 2)
    gathered_b[row] = second_ref[...]
    passed_s0 = relay(share_0, lambda k, q: full_0.at[k, q], share_sems(0))
    spread_2 = spread(fold_2, part_2, core_2, half_2, take_2, 2)
    exchange_1 = exchange(strip_sum(spread_1, half_1, take_1), mix_1, 1)
    arrive(passed_s0)

    gram = whole(full_0)
    pieces = 4
    width = panel_width // pieces
    columns = [gram[width * j :, width * j : width * (j + 1)] for j in range(pieces)]
    uppers, inverses, unders = [], [], []

    def factor(b):
        upper, inverse = eliminate(columns[b][:width], work_ref, out_ref)
        under = None
        if b < pieces - 1:
            under = dot_nt(columns[b][width:], inverse, HIGHEST)
            for j in range(b + 1, pieces):
                o = (j - b - 1) * width
                columns[j] = columns[j] - dot_nt(under[o:], under[o : o + width], HIGHEST)
        uppers.append(upper)
        inverses.append(inverse)
        unders.append(under)

    passed_2 = relay(gather_2, slots_b, gather_sems(1))
    factor(0)
    exchange_2 = exchange(strip_sum(spread_2, half_2, take_2), mix_2, 2)
    arrive(passed_2)
    product(gathered_b, send_b)
    scatter_2 = scatter(send_b, get_b, 1)
    share_1 = share(exchange_1, mix_1, full_1, 1)
    factor(1)
    share_2 = share(exchange_2, mix_2, full_2, 2)
    passed_s1 = relay(share_1, lambda k, q: full_1.at[k, q], share_sems(1))
    factor(2)
    passed_s2 = relay(share_2, lambda k, q: full_2.at[k, q], share_sems(2))
    factor(3)

    identity = (lax.broadcasted_iota(jnp.int32, (width, panel_width), 1)
                - lax.broadcasted_iota(jnp.int32, (width, panel_width), 0))
    for b in range(pieces):
        target = (identity == b * width).astype(F32)
        for e in range(b):
            o = (b - e - 1) * width
            target = target - dot_nn(unders[e][o : o + width], lower_ref[e * width : (e + 1) * width, :], HIGHEST)
        lower_ref[b * width : (b + 1) * width, :] = dot_nn(inverses[b], target, HIGHEST)
    for b in range(pieces):
        parts = [jnp.zeros((width, b * width), F32)] if b else []
        parts.append(uppers[b])
        if b < pieces - 1:
            parts.append(unders[b].T)
        upper_out[b * width : (b + 1) * width, :] = jnp.concatenate(parts, axis=1)

    collect(scatter_2, get_b, third_ref)
    arrive(passed_s1)
    cross_out[:, :panel_width] = whole(full_1)
    arrive(passed_s2)
    cross_out[:, panel_width:] = whole(full_2)
    for copy in everything:
        copy.wait_send()


def project(lower_ref, upper_ref, cross_ref, first_ref, second_ref, third_ref, panel_ref,
            upper_out, coef_out, proj_out):
    upper_out[...] = upper_ref[...]
    width = panel_ref.shape[1]
    lower_inverse = lower_ref[...]
    for j, source in enumerate((first_ref, second_ref, third_ref)):
        here = slice(j * width, (j + 1) * width)
        coefficients = dot_nn(lower_inverse, cross_ref[:, here], HIGHEST)
        coef_out[:, here] = coefficients
        weights = dot_tn(lower_inverse, coefficients, HIGHEST)
        weight_high = weights.astype(BF16)
        weight_rest = (weights - weight_high.astype(F32)).astype(BF16)
        removed = dot_nn(panel_ref[...], weight_high) + dot_nn(panel_ref[...], weight_rest)
        proj_out[:, here] = (source[...].astype(F32) - removed).astype(BF16)


def shards(n_row, n_col, sparse_tiles, tile_columns, block_counts, krylov_first, panel_block):
    row_blocks, degree, tile, _ = sparse_tiles.shape
    rows_dev, width = panel_block.shape
    strip = width // n_row
    n_chip = n_row // 2
    vmem = pl.BlockSpec(memory_space=pltpu.VMEM)
    smem = pl.BlockSpec(memory_space=pltpu.SMEM)
    dma = pltpu.SemaphoreType.DMA
    shape = jax.ShapeDtypeStruct
    spans = (1, 1, 2)
    call = pl.pallas_call(
        functools.partial(body, n_row, n_col, degree, row_blocks, tile),
        out_shape=[
            shape((width, width), F32),
            shape((width, width), F32),
            shape((width, 3 * width), F32),
            shape((rows_dev, width), BF16),
            shape((rows_dev, width), BF16),
        ],
        in_specs=[pl.BlockSpec(memory_space=pl.ANY), smem, smem, vmem, vmem],
        out_specs=[vmem] * 5,
        scratch_shapes=[
            pltpu.VMEM(sparse_tiles.shape, BF16),
            pltpu.VMEM((row_blocks * tile, n_row * rows_dev), BF16),
            pltpu.VMEM((n_row, rows_dev, width), BF16),
            pltpu.VMEM((n_row, rows_dev, width), BF16),
            pltpu.VMEM((n_col, rows_dev, width), BF16),
            pltpu.VMEM((row_blocks * tile, width), F32),
            *[pltpu.VMEM((n_col, rows_dev, width), BF16)] * 4,
            pltpu.VMEM((2, n_chip, width, rows_dev), BF16),
            pltpu.VMEM((n_chip, width, rows_dev), BF16),
            pltpu.VMEM((n_chip, width, rows_dev), BF16),
            pltpu.VMEM((n_chip, width, rows_dev), BF16),
            pltpu.VMEM((width, rows_dev), BF16),
            *[pltpu.VMEM((2, n_chip, strip, k * width), F32) for k in spans],
            *[pltpu.VMEM((n_chip, strip, k * width), F32) for k in spans],
            *[pltpu.VMEM((n_chip, strip, k * width), F32) for k in spans],
            *[pltpu.VMEM((n_chip, strip, k * width), F32) for k in spans],
            *[pltpu.VMEM((n_col, strip, k * width), F32) for k in spans],
            *[pltpu.VMEM((2, n_chip, strip, k * width), F32) for k in spans],
            pltpu.VMEM((width // 4, width // 2), F32),
            pltpu.VMEM((width // 4, width // 2), F32),
            dma,
            *[dma((2, n_chip))] * 4,
            *[dma((n_col,))] * 2,
            *[dma((2, n_col))] * 2,
            *[dma((4,))] * 2,
            *[dma((4, n_chip))] * 2,
            *[dma((3, n_col))] * 2,
            *[dma((3, n_chip))] * 4,
        ],
        compiler_params=pltpu.CompilerParams(collective_id=0, has_side_effects=True),
        name="range_finder",
    )
    lower, upper, cross, second, third = call(
        sparse_tiles, tile_columns, block_counts.reshape(1, row_blocks), krylov_first, panel_block
    )
    return tuple(pl.pallas_call(
        project,
        out_shape=[
            shape((width, width), F32),
            shape((width, 3 * width), F32),
            shape((rows_dev, 3 * width), BF16),
        ],
        in_specs=[vmem] * 7,
        out_specs=[vmem] * 3,
        name="project",
    )(lower, upper, cross, krylov_first, second, third, panel_block))


def solution(mesh):
    n_row, n_col = mesh.shape["row"], mesh.shape["col"]
    in_specs = (
        P(("row", "col"), None, None, None),
        P(("row", "col"), None),
        P(("row", "col")),
        P(("row", "col"), None),
        P(("row", "col"), None),
    )
    out_specs = (P(), P(), P(("row", "col"), None))
    return jax.shard_map(
        functools.partial(shards, n_row, n_col), mesh=mesh, in_specs=in_specs, out_specs=out_specs, check_vma=False
    )
```

```python
import functools

import jax
import jax.numpy as jnp
from jax import lax
from jax.experimental import pallas as pl
from jax.experimental.pallas import tpu as pltpu
from jax.sharding import PartitionSpec as P

HIGHEST = lax.Precision.HIGHEST
F32 = jnp.float32
BF16 = jnp.bfloat16


def dot_nn(a, b, precision=None):
    return lax.dot_general(a, b, (((1,), (0,)), ((), ())), precision=precision, preferred_element_type=F32)


def dot_nt(a, b, precision=None):
    return lax.dot_general(a, b, (((1,), (1,)), ((), ())), precision=precision, preferred_element_type=F32)


def dot_tn(a, b, precision=None):
    return lax.dot_general(a, b, (((0,), (0,)), ((), ())), precision=precision, preferred_element_type=F32)


def eliminate(diag, work_ref, out_ref):
    width = diag.shape[0]
    low = lax.broadcasted_iota(jnp.int32, (width, width), 0)
    high = lax.broadcasted_iota(jnp.int32, (width, width), 1)
    work_ref[...] = jnp.concatenate([diag, (low == high).astype(F32)], axis=1)
    sub = lax.broadcasted_iota(jnp.int32, (8, 2 * width), 0)

    def group(index, carry):
        rows = work_ref[:8, :]
        scale = jnp.zeros((8, 2 * width), F32)
        spread = [jnp.broadcast_to(rows[:, k : k + 1], (8, 2 * width)) for k in range(8)]
        for i in range(8):
            inverse = 1.0 / jnp.broadcast_to(spread[i][i : i + 1, :], (8, 2 * width))
            factor = jnp.where(sub > i, spread[i] * inverse, 0.0)
            scale = jnp.where(sub == i, inverse, scale)
            for k in range(i + 1, 8):
                spread[k] = spread[k] - factor * spread[k][i : i + 1, :]
            rows = rows - factor * rows[i : i + 1, :]
        scaled = rows * scale
        rest = work_ref[...] - dot_tn(scaled[:, :width], rows, HIGHEST)
        at = pl.multiple_of(index * 8, 8)
        out_ref[pl.ds(at, 8), :] = pltpu.roll(rows * jnp.sqrt(scale), index * 8, 1)
        rest = pltpu.roll(rest, 2 * width - 8, 1)
        work_ref[: width - 8, :] = rest[8:, :]
        work_ref[width - 8 :, :] = jnp.zeros((8, 2 * width), F32)
        return carry

    lax.fori_loop(0, width // 8, group, 0)
    both = out_ref[...]
    upper = jnp.where(high >= low, both[:, :width], 0.0)
    inverse = jnp.where(high <= low, both[:, width:], 0.0)
    return upper, inverse


def over_chunks(total, chunk, run):
    if total <= chunk:
        run(0, total)
    else:
        def one(index, carry):
            run(pl.multiple_of(index * chunk, chunk), chunk)
            return carry

        lax.fori_loop(0, total // chunk, one, 0)


def body(n_row, n_col, degree, row_blocks, tile,
         tiles_hbm, columns_ref, counts_ref, first_ref, panel_ref,
         lower_ref, upper_out, cross_out, second_ref, third_ref,
         tiles_ref, dense_ref, gathered_a, gathered_b, panels_ref, sums_ref, send_a, send_b, get_a, get_b,
         parts, cores, halves, takes, mixes, fulls, turned_ref,
         work_ref, out_ref,
         tile_sem, gs_sem, gr_sem, gfs_sem, gfr_sem, ps_sem, pr_sem, ss_sem, sr_sem,
         cs_sem, cr_sem, rs_sem, rr_sem, xs_sem, xr_sem, as_sem, ar_sem, afs_sem, afr_sem):
    row = lax.axis_index("row")
    col = lax.axis_index("col")
    panel_width = panel_ref.shape[1]
    rows_dev = panel_ref.shape[0]
    n_chip = n_row // 2
    chip = row // 2
    core = lax.rem(row, 2)
    other = 1 - core
    partner = chip * 2 + other
    mesh_type = pl.DeviceIdType.MESH

    load_tiles = pltpu.make_async_copy(tiles_hbm, tiles_ref, tile_sem)
    load_tiles.start()

    def ahead(step):
        return lax.rem(chip + step, n_chip)

    def behind(step):
        return lax.rem(chip + n_chip - step, n_chip)

    def col_peer(step):
        return lax.rem(col + step, n_col)

    barrier = pltpu.get_barrier_semaphore()
    pl.semaphore_signal(barrier, inc=1, device_id=(partner, col), device_id_type=mesh_type)
    for step in range(1, n_chip):
        pl.semaphore_signal(barrier, inc=1, device_id=(ahead(step) * 2 + core, col), device_id_type=mesh_type)
    for step in range(1, n_col):
        pl.semaphore_signal(barrier, inc=1, device_id=(row, col_peer(step)), device_id_type=mesh_type)

    everything = []

    def begin(copies):
        for copy in copies:
            copy.start()
        everything.extend(copies)
        return copies

    def arrive(copies):
        for copy in copies:
            copy.wait_recv()

    def to_partner(source, target, send_sem, recv_sem):
        return pltpu.make_async_remote_copy(
            src_ref=source, dst_ref=target, send_sem=send_sem, recv_sem=recv_sem,
            device_id=(partner, col), device_id_type=mesh_type)

    def over_chips(source, target, send_sem, recv_sem):
        return [
            pltpu.make_async_remote_copy(
                src_ref=source(step), dst_ref=target(step),
                send_sem=send_sem.at[step], recv_sem=recv_sem.at[step],
                device_id=(ahead(step) * 2 + core, col), device_id_type=mesh_type)
            for step in range(1, n_chip)
        ]

    def over_col(source, target, send_sem, recv_sem):
        return [
            pltpu.make_async_remote_copy(
                src_ref=source(step), dst_ref=target(step),
                send_sem=send_sem.at[step], recv_sem=recv_sem.at[step],
                device_id=(row, col_peer(step)), device_id_type=mesh_type)
            for step in range(1, n_col)
        ]

    def gather(source, slots, sems):
        send, recv, pass_send, pass_recv = sems
        copies = begin(over_chips(lambda s: source, lambda s: slots(core, chip), send, recv))
        near = begin([to_partner(source, slots(core, chip), pass_send.at[0], pass_recv.at[0])])
        return copies, near

    def relay(state, slots, sems):
        copies, near = state
        send, recv, pass_send, pass_recv = sems
        passed = list(near)
        for step, copy in enumerate(copies, start=1):
            copy.wait_recv()
            here = slots(core, behind(step))
            passed += begin([to_partner(here, here, pass_send.at[step], pass_recv.at[step])])
        return passed

    def gather_sems(index):
        return gs_sem.at[index], gr_sem.at[index], gfs_sem.at[index], gfr_sem.at[index]

    def share_sems(index):
        return as_sem.at[index], ar_sem.at[index], afs_sem.at[index], afr_sem.at[index]

    def fold(part_ref, core_ref, index):
        return begin([to_partner(part_ref.at[other], core_ref, cs_sem.at[index], cr_sem.at[index])])

    def spread(folded, part_ref, core_ref, half_ref, take_ref, index):
        arrive(folded)
        half_ref[...] = (part_ref[core].astype(F32) + core_ref[...].astype(F32)).astype(half_ref.dtype)
        return begin(over_chips(lambda s: half_ref.at[ahead(s)], lambda s: take_ref.at[s],
                                rs_sem.at[index], rr_sem.at[index]))

    def strip_sum(copies, half_ref, take_ref):
        total = half_ref[chip].astype(F32)
        arrive(copies)
        for step in range(1, n_chip):
            total = total + take_ref[step].astype(F32)
        return total

    def put(value, part_ref, at):
        width = value.shape[1]
        part_ref[:, :, :, at : at + width] = value.reshape(part_ref.shape[:3] + (width,))

    def exchange(total, mix_ref, index):
        mix_ref[col] = total
        return begin(over_col(lambda s: mix_ref.at[col], lambda s: mix_ref.at[col],
                              xs_sem.at[index], xr_sem.at[index]))

    def share(copies, mix_ref, full_ref, index):
        arrive(copies)
        total = mix_ref[0]
        for c in range(1, n_col):
            total = total + mix_ref[c]
        full_ref[core, chip] = total
        return gather(full_ref.at[core, chip], lambda k, q: full_ref.at[k, q], share_sems(index))

    def whole(full_ref):
        return full_ref[...].reshape(panel_width, full_ref.shape[3])

    def product(gathered_ref, send_ref):
        right = gathered_ref[...].reshape(n_row * rows_dev, panel_width)

        def run(at, size):
            sums_ref[pl.ds(at, size), :] = dot_nn(dense_ref[pl.ds(at, size), :], right)

        over_chunks(row_blocks * tile, 4 * tile, run)
        for c in range(n_col):
            send_ref[c] = sums_ref[c * rows_dev : (c + 1) * rows_dev, :].astype(BF16)

    def scatter(send_ref, get_ref, index):
        return begin(over_col(lambda s: send_ref.at[col_peer(s)], lambda s: get_ref.at[s],
                              ss_sem.at[index], sr_sem.at[index]))

    def collect(copies, get_ref, result_ref):
        own = sums_ref[pl.ds(pl.multiple_of(col * rows_dev, 8), rows_dev), :]
        arrive(copies)
        for step in range(1, n_col):
            own = own + get_ref[step].astype(F32)
        result_ref[...] = own.astype(BF16)

    def slots_a(k, q):
        return gathered_a.at[q * 2 + k]

    def slots_b(k, q):
        return gathered_b.at[q * 2 + k]

    def stage(index, value):
        put(value, parts.at[index], 0)
        return fold(parts.at[index], cores.at[index], index)

    def spread_stage(index, folded):
        return spread(folded, parts.at[index], cores.at[index], halves.at[index], takes.at[index], index)

    def exchange_stage(index, copies):
        return exchange(strip_sum(copies, halves.at[index], takes.at[index]), mixes.at[index], index)

    def full_slots(index):
        return lambda k, q: fulls.at[index, k, q]

    def share_stage(index, copies):
        return share(copies, mixes.at[index], fulls.at[index], index)

    def relay_stage(index, state):
        return relay(state, full_slots(index), share_sems(index))

    panel = panel_ref[...]
    put(dot_tn(panel, panel), parts.at[0], 0)
    pl.semaphore_wait(barrier, n_chip + n_col - 1)

    gather_1 = gather(first_ref, slots_a, gather_sems(0))
    fold_0 = fold(parts.at[0], cores.at[0], 0)
    panels = begin(over_col(lambda s: panel_ref, lambda s: panels_ref.at[col], ps_sem, pr_sem))
    gathered_a[row] = first_ref[...]
    panels_ref[col] = panel_ref[...]

    load_tiles.wait()
    column_blocks = n_row * rows_dev // tile

    def place(b):
        for j in range(column_blocks):
            slot = jnp.int32(0)
            live = jnp.int32(0)
            for k in range(degree):
                hit = jnp.logical_and(columns_ref[b, k] == j, k < counts_ref[0, b])
                slot = jnp.where(hit, k, slot)
                live = jnp.where(hit, 1, live)
            value = tiles_ref[b, slot]
            dense_ref[pl.ds(b * tile, tile), j * tile : (j + 1) * tile] = jnp.where(
                live > 0, value, jnp.zeros_like(value))

    if row_blocks <= 4:
        for b in range(row_blocks):
            place(b)
    else:
        def place_one(b, carry):
            place(b)
            return carry

        lax.fori_loop(0, row_blocks, place_one, 0)

    spread_0 = spread_stage(0, fold_0)
    passed_1 = relay(gather_1, slots_a, gather_sems(0))
    fold_1 = stage(1, dot_tn(panel, first_ref[...]))
    arrive(passed_1)
    product(gathered_a, send_a)
    scatter_1 = scatter(send_a, get_a, 0)
    exchange_0 = exchange_stage(0, spread_0)
    spread_1 = spread_stage(1, fold_1)
    collect(scatter_1, get_a, second_ref)
    gather_2 = gather(second_ref, slots_b, gather_sems(1))
    fold_2 = stage(2, dot_tn(panel, second_ref[...]))
    gathered_b[row] = second_ref[...]
    exchange_1 = exchange_stage(1, spread_1)
    share_0 = share_stage(0, exchange_0)
    spread_2 = spread_stage(2, fold_2)
    arrive(panels)
    turned_ref[...] = panels_ref[...].reshape(n_col * rows_dev, panel_width).T
    passed_2 = relay(gather_2, slots_b, gather_sems(1))
    exchange_2 = exchange_stage(2, spread_2)
    passed_s0 = relay_stage(0, share_0)
    arrive(passed_2)
    product(gathered_b, send_b)
    fold_3 = stage(3, dot_nn(turned_ref[...], send_b[...].reshape(n_col * rows_dev, panel_width)))
    scatter_2 = scatter(send_b, get_b, 1)
    spread_3 = spread_stage(3, fold_3)
    share_1 = share_stage(1, exchange_1)
    arrive(passed_s0)

    gram = whole(fulls.at[0])
    pieces = 4
    width = panel_width // pieces
    columns = [gram[width * j :, width * j : width * (j + 1)] for j in range(pieces)]
    uppers, inverses, unders = [], [], []

    def factor(b):
        upper, inverse = eliminate(columns[b][:width], work_ref, out_ref)
        under = None
        if b < pieces - 1:
            under = dot_nt(columns[b][width:], inverse, HIGHEST)
            for j in range(b + 1, pieces):
                o = (j - b - 1) * width
                columns[j] = columns[j] - dot_nt(under[o:], under[o : o + width], HIGHEST)
        uppers.append(upper)
        inverses.append(inverse)
        unders.append(under)

    factor(0)
    exchange_3 = exchange_stage(3, spread_3)
    passed_s1 = relay_stage(1, share_1)
    share_2 = share_stage(2, exchange_2)
    factor(1)
    share_3 = share_stage(3, exchange_3)
    passed_s2 = relay_stage(2, share_2)
    factor(2)
    passed_s3 = relay_stage(3, share_3)
    factor(3)

    identity = (lax.broadcasted_iota(jnp.int32, (width, panel_width), 1)
                - lax.broadcasted_iota(jnp.int32, (width, panel_width), 0))
    for b in range(pieces):
        target = (identity == b * width).astype(F32)
        for e in range(b):
            o = (b - e - 1) * width
            target = target - dot_nn(unders[e][o : o + width], lower_ref[e * width : (e + 1) * width, :], HIGHEST)
        lower_ref[b * width : (b + 1) * width, :] = dot_nn(inverses[b], target, HIGHEST)
    for b in range(pieces):
        parts = [jnp.zeros((width, b * width), F32)] if b else []
        parts.append(uppers[b])
        if b < pieces - 1:
            parts.append(unders[b].T)
        upper_out[b * width : (b + 1) * width, :] = jnp.concatenate(parts, axis=1)

    collect(scatter_2, get_b, third_ref)
    for index, passed in enumerate((passed_s1, passed_s2, passed_s3)):
        arrive(passed)
        cross_out[:, index * panel_width : (index + 1) * panel_width] = whole(fulls.at[index + 1])
    for copy in everything:
        copy.wait_send()


def project(lower_ref, upper_ref, cross_ref, first_ref, second_ref, third_ref, panel_ref,
            upper_out, coef_out, proj_out):
    block = pl.program_id(0)

    @pl.when(block == 0)
    def _():
        upper_out[...] = upper_ref[...]

    lower_inverse = lower_ref[...]
    coefficients = dot_nn(lower_inverse, cross_ref[...], HIGHEST)
    coef_out[...] = coefficients
    weights = dot_tn(lower_inverse, coefficients, HIGHEST)
    weight_high = weights.astype(BF16)
    weight_rest = (weights - weight_high.astype(F32)).astype(BF16)
    removed = dot_nn(panel_ref[...], weight_high) + dot_nn(panel_ref[...], weight_rest)
    source = jnp.where(block == 0, first_ref[...], jnp.where(block == 1, second_ref[...], third_ref[...]))
    proj_out[...] = (source.astype(F32) - removed).astype(BF16)


def shards(n_row, n_col, sparse_tiles, tile_columns, block_counts, krylov_first, panel_block):
    row_blocks, degree, tile, _ = sparse_tiles.shape
    rows_dev, width = panel_block.shape
    strip = width // n_row
    n_chip = n_row // 2
    vmem = pl.BlockSpec(memory_space=pltpu.VMEM)
    smem = pl.BlockSpec(memory_space=pltpu.SMEM)
    dma = pltpu.SemaphoreType.DMA
    shape = jax.ShapeDtypeStruct
    call = pl.pallas_call(
        functools.partial(body, n_row, n_col, degree, row_blocks, tile),
        out_shape=[
            shape((width, width), F32),
            shape((width, width), F32),
            shape((width, 3 * width), F32),
            shape((rows_dev, width), BF16),
            shape((rows_dev, width), BF16),
        ],
        in_specs=[pl.BlockSpec(memory_space=pl.ANY), smem, smem, vmem, vmem],
        out_specs=[vmem] * 5,
        scratch_shapes=[
            pltpu.VMEM(sparse_tiles.shape, BF16),
            pltpu.VMEM((row_blocks * tile, n_row * rows_dev), BF16),
            pltpu.VMEM((n_row, rows_dev, width), BF16),
            pltpu.VMEM((n_row, rows_dev, width), BF16),
            pltpu.VMEM((n_col, rows_dev, width), BF16),
            pltpu.VMEM((row_blocks * tile, width), F32),
            *[pltpu.VMEM((n_col, rows_dev, width), BF16)] * 4,
            pltpu.VMEM((4, 2, n_chip, strip, width), F32),
            *[pltpu.VMEM((4, n_chip, strip, width), F32)] * 3,
            pltpu.VMEM((4, n_col, strip, width), F32),
            pltpu.VMEM((4, 2, n_chip, strip, width), F32),
            pltpu.VMEM((width, n_col * rows_dev), BF16),
            pltpu.VMEM((width // 4, width // 2), F32),
            pltpu.VMEM((width // 4, width // 2), F32),
            dma,
            *[dma((2, n_chip))] * 4,
            *[dma((n_col,))] * 2,
            *[dma((2, n_col))] * 2,
            *[dma((4,))] * 2,
            *[dma((4, n_chip))] * 2,
            *[dma((4, n_col))] * 2,
            *[dma((4, n_chip))] * 4,
        ],
        compiler_params=pltpu.CompilerParams(collective_id=0, has_side_effects=True),
        name="range_finder",
    )
    lower, upper, cross, second, third = call(
        sparse_tiles, tile_columns, block_counts.reshape(1, row_blocks), krylov_first, panel_block
    )
    return tuple(pl.pallas_call(
        project,
        out_shape=[
            shape((width, width), F32),
            shape((width, 3 * width), F32),
            shape((rows_dev, 3 * width), BF16),
        ],
        grid=(3,),
        in_specs=[
            pl.BlockSpec((width, width), lambda j: (0, 0)),
            pl.BlockSpec((width, width), lambda j: (0, 0)),
            pl.BlockSpec((width, width), lambda j: (0, j)),
            *[pl.BlockSpec((rows_dev, width), lambda j: (0, 0))] * 4,
        ],
        out_specs=[
            pl.BlockSpec((width, width), lambda j: (0, 0)),
            pl.BlockSpec((width, width), lambda j: (0, j)),
            pl.BlockSpec((rows_dev, width), lambda j: (0, j)),
        ],
        name="project",
    )(lower, upper, cross, krylov_first, second, third, panel_block))


def solution(mesh):
    n_row, n_col = mesh.shape["row"], mesh.shape["col"]
    in_specs = (
        P(("row", "col"), None, None, None),
        P(("row", "col"), None),
        P(("row", "col")),
        P(("row", "col"), None),
        P(("row", "col"), None),
    )
    out_specs = (P(), P(), P(("row", "col"), None))
    return jax.shard_map(
        functools.partial(shards, n_row, n_col), mesh=mesh, in_specs=in_specs, out_specs=out_specs, check_vma=False
    )
```
